32 devices in a mesh: tile: 4 (over y, x), orient: 8 (over z, core).
Axes of the slice: x: 2, y: 2, z: 4, core: 2. Of those that a mesh axis runs over, the one named last changes fastest.
Arguments:
- micrograph_tiles: bfloat16 [8, 512, 512], P('tile'), as said below
- tile_offsets: int32 [8, 2], P('tile'), may hold values from 0 to 3584
- library: bfloat16 [32, 8, 128, 128], P('tile', 'orient'), as said below
- orient_ids: int32 [8, 2], P('orient'), may hold values from 0 to 31
Outputs:
- peak_score: float32 [8, 384, 384], P('tile')
- z_score: float32 [8, 384, 384], P('tile')
The draws below stay inside these ranges and needn't reach their ends.
Inputs may be any that keep to these rules, and one draw needn't show every extreme that they name: `micrograph_tiles`: real-valued pixel intensities of the tiles. `library`: real-valued projection densities.
All inputs are finite; a program needn't handle non-finite values.
Results may differ from the reference program's by a relative error of at most 0.0095.
Values may be sent and summed in bfloat16 or wider, within the bound.
A program may use at most 64 MiB of HBM per device.

```python
import math
import jax
import jax.numpy as jnp
from jax import lax

PAD = 512
TPL = 128
VALID = 384
STEPS = 2
TILES = 8
LIB = 32
SHARDS = 8
SEARCH = 16


def draw_micrograph_tiles(key, part):
    subkeys = jax.random.split(key, 4)
    base_draw = jax.random.truncated_normal(subkeys[0], -6.0, 6.0, (TILES, PAD, PAD), jnp.float32)
    ramp_values = jnp.arange(TILES, dtype=jnp.float32) / max(TILES - 1, 1)
    tile_scale = jnp.exp(math.log(3.0) * ramp_values + jax.random.uniform(subkeys[1], (TILES,), jnp.float32, 0.0, math.log(4.0)))
    row_scale = jnp.exp(jax.random.uniform(subkeys[2], (TILES, PAD, 1), jnp.float32, 0.0, math.log(10.0)))
    col_scale = jnp.exp(jax.random.uniform(subkeys[3], (TILES, 1, PAD), jnp.float32, 0.0, math.log(10.0)))
    return (base_draw * tile_scale[:, None, None] * row_scale * col_scale).astype(jnp.bfloat16)


def draw_library(key, part):
    subkeys = jax.random.split(key, 3)
    base_draw = jax.random.truncated_normal(subkeys[0], -6.0, 6.0, (LIB, SHARDS, TPL, TPL), jnp.float32)
    row_scale = jnp.exp(jax.random.uniform(subkeys[1], (LIB, SHARDS, TPL, 1), jnp.float32, 0.0, math.log(10.0)))
    col_scale = jnp.exp(jax.random.uniform(subkeys[2], (LIB, SHARDS, 1, TPL), jnp.float32, 0.0, math.log(10.0)))
    return (base_draw * row_scale * col_scale).astype(jnp.bfloat16)


def with_ends(drawn, key, smallest, top_value):
    extent = drawn.shape
    place = [jax.random.randint(jax.random.fold_in(key, axis), (), 0, extent[axis]) for axis in range(len(extent))]
    drawn = drawn.at[tuple(place)].set(smallest)
    longest = extent.index(max(extent))
    place[longest] = (place[longest] + 1) % extent[longest]
    return drawn.at[tuple(place)].set(top_value)


def setup_inputs(seed: int = 0) -> dict:
    seeds = jax.random.split(jax.random.key(seed), 5)
    micrograph_tiles = draw_micrograph_tiles(jax.random.fold_in(seeds[4], 71), 0)
    tile_offsets = with_ends(jax.random.randint(seeds[1], (TILES, 2), 0, 3585), jax.random.fold_in(seeds[1], 1), 0, 3584).astype(jnp.int32)
    library = draw_library(jax.random.fold_in(seeds[4], 71), 0)
    orient_ids = with_ends(jax.random.randint(seeds[3], (SHARDS, STEPS), 0, LIB), jax.random.fold_in(seeds[3], 1), 0, LIB - 1).astype(jnp.int32)
    return {"micrograph_tiles": micrograph_tiles, "tile_offsets": tile_offsets, "library": library, "orient_ids": orient_ids}


AMPLITUDE = 0.07
DEFOCUS_BASE = 100.0
DEFOCUS_TILT = 0.002
FLOOR_SHARE = 0.25

def dft_tables(length):
    counter = jnp.arange(length, dtype=jnp.int32)
    product = counter[:, None] * counter[None, :] % length
    angle_table = product.astype(jnp.float32) * (2.0 * math.pi / length)
    return (jnp.cos(angle_table).astype(jnp.bfloat16), jnp.sin(angle_table).astype(jnp.bfloat16))

def frequency_squares(length):
    counter = jnp.arange(length, dtype=jnp.int32)
    signed = jnp.where(counter < length // 2, counter, counter - length)
    frequency = signed.astype(jnp.float32) / length
    return frequency[:, None] * frequency[:, None] + frequency[None, :] * frequency[None, :]

def batched(spec, left_op, right_op):
    return jnp.einsum(spec, left_op.astype(jnp.float32), right_op.astype(jnp.float32))

def forward_tiles(images, cosine_table, sine_table):
    half_real = batched('tij,jk->tik', images, cosine_table).astype(jnp.bfloat16)
    half_imag = (-batched('tij,jk->tik', images, sine_table)).astype(jnp.bfloat16)
    spec_real = batched('ij,tjk->tik', cosine_table, half_real) + batched('ij,tjk->tik', sine_table, half_imag)
    spec_imag = batched('ij,tjk->tik', cosine_table, half_imag) - batched('ij,tjk->tik', sine_table, half_real)
    return (spec_real, spec_imag)

def tile_filters(tile_offsets, whiten, length):
    squares_freq = frequency_squares(length)
    offsets = tile_offsets.astype(jnp.float32)
    defocus = DEFOCUS_BASE + DEFOCUS_TILT * (offsets[:, 0] - offsets[:, 1])
    phase_angle = math.pi * defocus[:, None, None] * squares_freq[None]
    contrast = -(math.sqrt(1.0 - AMPLITUDE * AMPLITUDE) * jnp.sin(phase_angle) + AMPLITUDE * jnp.cos(phase_angle))
    center = jnp.where(squares_freq > 0.0, 1.0, 0.0).astype(jnp.float32)
    return contrast * (whiten * center)[None]

def template_spectrum(template, cosine_table, sine_table):
    pattern_size = template.shape[0]
    tpl_real = jnp.dot(template, cosine_table[:pattern_size], preferred_element_type=jnp.float32).astype(jnp.bfloat16)
    tpl_imag = (-jnp.dot(template, sine_table[:pattern_size], preferred_element_type=jnp.float32)).astype(jnp.bfloat16)
    col_cos = cosine_table[:, :pattern_size]
    col_sin = sine_table[:, :pattern_size]
    base_real = jnp.dot(col_cos, tpl_real, preferred_element_type=jnp.float32) + jnp.dot(col_sin, tpl_imag, preferred_element_type=jnp.float32)
    base_imag = jnp.dot(col_cos, tpl_imag, preferred_element_type=jnp.float32) - jnp.dot(col_sin, tpl_real, preferred_element_type=jnp.float32)
    return (base_real, base_imag)

def correlate(base_real, base_imag, filters, white_real, white_imag, cosine_table, sine_table, valid_rows):
    length = cosine_table.shape[0]
    filt_real = base_real[None] * filters
    filt_imag = base_imag[None] * filters
    energy = lax.optimization_barrier(jnp.mean(filt_real * filt_real + filt_imag * filt_imag, axis=(1, 2), keepdims=True))
    norm_scale = lax.rsqrt(energy + 1e-06)
    norm_real = (filt_real * norm_scale).astype(jnp.bfloat16).astype(jnp.float32)
    norm_imag = (filt_imag * norm_scale).astype(jnp.bfloat16).astype(jnp.float32)
    wide_real = white_real.astype(jnp.float32)
    wide_imag = white_imag.astype(jnp.float32)
    prod_real = (wide_real * norm_real + wide_imag * norm_imag).astype(jnp.bfloat16)
    prod_imag = (wide_imag * norm_real - wide_real * norm_imag).astype(jnp.bfloat16)
    row_cos = cosine_table[:valid_rows]
    row_sin = sine_table[:valid_rows]
    mid_real = (batched('ij,tjk->tik', row_cos, prod_real) - batched('ij,tjk->tik', row_sin, prod_imag)).astype(jnp.bfloat16)
    mid_imag = (batched('ij,tjk->tik', row_cos, prod_imag) + batched('ij,tjk->tik', row_sin, prod_real)).astype(jnp.bfloat16)
    result = batched('tij,jk->tik', mid_real, cosine_table[:, :valid_rows]) - batched('tij,jk->tik', mid_imag, sine_table[:, :valid_rows])
    return result / length

def reference(micrograph_tiles, tile_offsets, library, orient_ids):
    cosine_table, sine_table = dft_tables(PAD)
    spec_real, spec_imag = forward_tiles(micrograph_tiles, cosine_table, sine_table)
    mean_power = lax.optimization_barrier(jnp.sum(spec_real * spec_real + spec_imag * spec_imag, axis=0)) / TILES
    whiten = lax.rsqrt(jnp.maximum(mean_power, FLOOR_SHARE * jnp.mean(mean_power)))
    white_real = (spec_real * whiten[None]).astype(jnp.bfloat16)
    white_imag = (spec_imag * whiten[None]).astype(jnp.bfloat16)
    filters = tile_filters(tile_offsets, whiten, PAD)
    shard_index = jnp.arange(SHARDS, dtype=jnp.int32)
    templates = library[orient_ids, shard_index[:, None]].reshape(SEARCH, TPL, TPL)

    def visit_template(state_tuple, template):
        running_peak, running_sum, squares = state_tuple
        base_real, base_imag = template_spectrum(template, cosine_table, sine_table)
        scores = correlate(base_real, base_imag, filters, white_real, white_imag, cosine_table, sine_table, VALID)
        return ((jnp.maximum(running_peak, scores), running_sum + scores, squares + scores * scores), None)
    initial = (jnp.full((TILES, VALID, VALID), -jnp.inf, jnp.float32), jnp.zeros((TILES, VALID, VALID), jnp.float32), jnp.zeros((TILES, VALID, VALID), jnp.float32))
    (running_peak, running_sum, squares), _ = lax.scan(visit_template, initial, templates)
    mean_score = running_sum / SEARCH
    variance = squares / SEARCH - mean_score * mean_score
    z_score = (running_peak - mean_score) * lax.rsqrt(variance + 1e-06)
    return (running_peak, z_score)
```

```python
import functools
import math

import jax
import jax.numpy as jnp
import numpy as np
from jax import lax
from jax.experimental import pallas as pl
from jax.experimental.pallas import tpu as pltpu
from jax.sharding import PartitionSpec as P

VALID = 384

AMPLITUDE = 0.07
DEFOCUS_BASE = 100.0
DEFOCUS_TILT = 0.002
FLOOR_SHARE = 0.25
MESH = pl.DeviceIdType.MESH
VMEM = pl.BlockSpec(memory_space=pltpu.VMEM)
SMEM = pl.BlockSpec(memory_space=pltpu.SMEM)
GRANT = 56 * 1024 * 1024


def tables(length, valid):
    half = length // 2
    rows = -(-(half + 1) // 16) * 16
    a_index = np.concatenate([np.arange(0, length, 2), np.arange(1, length, 2)])
    j_index = np.arange(length)
    b_index = np.arange(half + 1)

    def wave(function, left, right):
        return function((left[:, None] * right[None, :]) % length * (2.0 * np.pi / length))

    first = np.zeros((2, rows, length))
    first[0, : half + 1] = wave(np.cos, b_index, j_index)
    first[1, : half + 1] = -wave(np.sin, b_index, j_index)
    second_cos = wave(np.cos, j_index, a_index)
    second_sin = wave(np.sin, j_index, a_index)
    back = []
    for parity in range(2):
        cosine = wave(np.cos, a_index[parity * half : (parity + 1) * half], j_index[:half])
        sine = wave(np.sin, a_index[parity * half : (parity + 1) * half], j_index[:half])
        back.append(np.block([[cosine, sine], [-sine, cosine]]))
    count = np.full((half,), 2.0)
    count[0] = 1.0
    last_cos = wave(np.cos, j_index[:valid], b_index[:half]) * count / length
    last_sin = -wave(np.sin, j_index[:valid], b_index[:half]) * count / length
    last_sin[:, 0] = np.cos(np.pi * j_index[:valid]) / length
    last = np.concatenate([last_cos, last_sin], axis=1)

    signed = np.where(a_index < half, a_index, a_index - length) / length
    a_square = (signed * signed)[None, :]
    b_square = np.zeros((rows, 1))
    b_square[: half + 1, 0] = (b_index / length) ** 2
    weight = np.zeros((rows, 1))
    weight[: half + 1, 0] = 2.0
    weight[0, 0] = weight[half, 0] = 1.0

    def narrow(value):
        return np.asarray(value, np.float32).astype(jnp.bfloat16)

    return dict(
        first=narrow(first.reshape(2 * rows, length)),
        cos=narrow(second_cos),
        sin=narrow(second_sin),
        even=narrow(back[0]),
        odd=narrow(back[1]),
        last=narrow(last),
        a_square=a_square.astype(np.float32),
        b_square=b_square.astype(np.float32),
        weight=weight.astype(np.float32),
    )


def dot(left, right):
    return jnp.dot(left, right, preferred_element_type=jnp.float32)


def dot_nt(left, right):
    return lax.dot_general(
        left, right, (((1,), (1,)), ((), ())), preferred_element_type=jnp.float32
    )


def sine_of_turns(turns):
    part = turns - jnp.floor(turns + 0.5)
    mirrored = jnp.where(part > 0.0, 0.5, -0.5) - part
    part = jnp.where(jnp.abs(part) > 0.25, mirrored, part)
    angle = part * (2.0 * math.pi)
    square = angle * angle
    poly = -1.0 / 39916800.0
    for term in (1.0 / 362880.0, -1.0 / 5040.0, 1.0 / 120.0, -1.0 / 6.0, 1.0):
        poly = poly * square + term
    return angle * poly


def forward_kernel(
    ids_ref, off_ref, x_ref, lib_ref, first_ref, cos_ref, sin_ref, a_ref, b_ref,
    real_ref, imag_ref, con_ref, pow_ref, tpl_ref,
):
    core = lax.rem(lax.axis_index("orient"), 2)
    mine = lax.axis_index("tile")
    slots = lib_ref.shape[0]
    rows, length = real_ref.shape
    half = length // 2
    for step in range(tpl_ref.shape[0]):
        chosen = ids_ref[0, step]
        owner = chosen // slots
        picked = lib_ref[chosen - owner * slots, 0]
        keep = jnp.where(owner == mine, 1.0, 0.0).astype(jnp.float32)
        tpl_ref[step] = jnp.where(keep > 0.0, picked.astype(jnp.float32), 0.0).astype(jnp.bfloat16)
    halves = dot_nt(first_ref[...], x_ref[core]).astype(jnp.bfloat16)
    half_real, half_imag = halves[:rows], halves[rows:]
    spec_real = dot(half_real, cos_ref[...]) + dot(half_imag, sin_ref[...])
    spec_imag = dot(half_imag, cos_ref[...]) - dot(half_real, sin_ref[...])
    power = spec_real * spec_real + spec_imag * spec_imag
    pow_ref[0] = power[:, :half].astype(jnp.bfloat16)
    pow_ref[1] = power[:, half:].astype(jnp.bfloat16)
    s2 = a_ref[...] + b_ref[...]
    tilt = (off_ref[core, 0] - off_ref[core, 1]).astype(jnp.float32)
    defocus = DEFOCUS_BASE + DEFOCUS_TILT * tilt
    shift = math.asin(AMPLITUDE) / (2.0 * math.pi)
    contrast = -sine_of_turns(s2 * (0.5 * defocus) + shift)
    contrast = jnp.where(s2 > 0.0, contrast, 0.0)
    con_ref[...] = contrast
    real_ref[...] = spec_real * contrast
    imag_ref[...] = spec_imag * contrast


def exchange_kernel(
    n_tile, n_orient, pow_ref, tpl_ref, total_ref, all_ref,
    pair_in, half_out, half_in, done_out, done_in, tpl_in, held, send_sem, recv_sem,
):
    tile = lax.axis_index("tile")
    orient = lax.axis_index("orient")
    core = lax.rem(orient, 2)
    chip = orient // 2
    n_chip = n_orient // 2
    partner = (tile, chip * 2 + 1 - core)
    tiles = [(lax.rem(tile + k, n_tile), orient) for k in range(1, n_tile)]
    chips = [(tile, lax.rem(chip + k, n_chip) * 2 + core) for k in range(1, n_chip)]

    barrier = pltpu.get_barrier_semaphore()
    for device in [partner] + tiles + chips:
        pl.semaphore_signal(barrier, inc=1, device_id=device, device_id_type=MESH)
    pl.semaphore_wait(barrier, 1 + len(tiles) + len(chips))

    used = [0]

    def send(src, dst, device):
        at = used[0]
        used[0] += 1
        copy = pltpu.make_async_remote_copy(
            src_ref=src, dst_ref=dst, send_sem=send_sem.at[at], recv_sem=recv_sem.at[at],
            device_id=device, device_id_type=MESH,
        )
        copy.start()
        return copy

    pair = send(pow_ref.at[1 - core], pair_in, partner)
    picks = [send(tpl_ref, tpl_in.at[k], device) for k, device in enumerate(tiles)]
    pair.wait()
    mine = pow_ref[core].astype(jnp.float32) + pair_in[...].astype(jnp.float32)
    half_out[...] = mine.astype(jnp.bfloat16)
    sums = [send(half_out, half_in.at[k], device) for k, device in enumerate(tiles)]
    template = tpl_ref[...].astype(jnp.float32)
    for k, copy in enumerate(picks):
        copy.wait()
        template = template + tpl_in[k].astype(jnp.float32)
    held[core, chip] = template.astype(jnp.bfloat16)
    spread = [send(held.at[core, chip], held.at[core, chip], device) for device in chips]
    for copy in sums:
        copy.wait()
    total = half_out[...].astype(jnp.float32)
    for k in range(len(tiles)):
        total = total + half_in[k].astype(jnp.float32)
    done_out[...] = total
    last = send(done_out, done_in, partner)
    for copy in spread:
        copy.wait()
    swap = send(held.at[core], held.at[core], partner)
    total_ref[core] = total
    last.wait()
    total_ref[1 - core] = done_in[...]
    swap.wait()
    all_ref[...] = held[...]


def search_kernel(
    tiles, real_ref, imag_ref, con_ref, total_ref, tpl_ref, first_ref, cos_ref, sin_ref,
    even_ref, odd_ref, last_ref, weight_ref, out_ref,
    g_real, g_imag, g_energy, base_table, mids, peak, total_sum, squares,
):
    rows, length = real_ref.shape
    half = length // 2
    valid = last_ref.shape[0]
    groups, steps, size, _ = tpl_ref.shape
    weight = weight_ref[...]
    sides = [total_ref[side] / tiles for side in range(2)]
    mean = (jnp.sum(sides[0] * weight) + jnp.sum(sides[1] * weight)) / (length * length)
    floor = FLOOR_SHARE * mean
    for side in range(2):
        columns = slice(side * half, (side + 1) * half)
        whiten2 = 1.0 / jnp.maximum(sides[side], floor)
        contrast = con_ref[:, columns]
        g_real[:, columns] = real_ref[:, columns] * whiten2
        g_imag[:, columns] = imag_ref[:, columns] * whiten2
        g_energy[:, columns] = contrast * contrast * whiten2 * (weight / (length * length))
    base_table[:size, :length] = cos_ref[:size]
    base_table[:size, length:] = -sin_ref[:size]
    base_table[size:, :length] = sin_ref[:size]
    base_table[size:, length:] = cos_ref[:size]
    peak[...] = jnp.full_like(peak, -jnp.inf)
    total_sum[...] = jnp.zeros_like(total_sum)
    squares[...] = jnp.zeros_like(squares)

    def visit(group, carry):
        images = tpl_ref[group].reshape(steps * size, size)
        halves = dot_nt(first_ref[...], images).astype(jnp.bfloat16)
        scales = []
        for step in range(steps):
            columns = slice(step * size, (step + 1) * size)
            joined = jnp.concatenate([halves[:rows, columns], halves[rows:, columns]], axis=1)
            base = dot(joined, base_table[...])
            base_real, base_imag = base[:, :length], base[:, length:]
            energy = jnp.sum(g_energy[...] * (base_real * base_real + base_imag * base_imag))
            scales.append(lax.rsqrt(energy + 1e-06))
            prod_real = (g_real[...] * base_real + g_imag[...] * base_imag).astype(jnp.bfloat16)
            prod_imag = (g_imag[...] * base_real - g_real[...] * base_imag).astype(jnp.bfloat16)
            even = dot(
                jnp.concatenate([prod_real[:, :half], prod_imag[:, :half]], axis=1), even_ref[...]
            )
            odd = dot(
                jnp.concatenate([prod_real[:, half:], prod_imag[:, half:]], axis=1), odd_ref[...]
            )
            both, apart = even + odd, even - odd
            mid_real = jnp.concatenate([both[:, :half], apart[:, : valid - half]], axis=1)
            mid_imag = jnp.concatenate([both[:half, half:], apart[:half, half:valid]], axis=1)
            row = lax.broadcasted_iota(jnp.int32, (half, valid), 0)
            mid_imag = jnp.where(row == 0, mid_real[half : half + 1], mid_imag)
            place = slice(step * valid, (step + 1) * valid)
            mids[:half, place] = mid_real[:half].astype(jnp.bfloat16)
            mids[half:, place] = mid_imag.astype(jnp.bfloat16)
        found = dot(last_ref[...], mids[...])
        top, add, add2 = peak[...], total_sum[...], squares[...]
        for step in range(steps):
            score = found[:, step * valid : (step + 1) * valid] * scales[step]
            top = jnp.maximum(top, score)
            add = add + score
            add2 = add2 + score * score
        peak[...] = top
        total_sum[...] = add
        squares[...] = add2
        return carry

    lax.fori_loop(0, groups, visit, 0)
    searched = groups * steps
    mean_score = total_sum[...] / searched
    variance = squares[...] / searched - mean_score * mean_score
    z_score = (peak[...] - mean_score) * lax.rsqrt(variance + 1e-06)
    out_ref[0] = peak[...].T.astype(jnp.bfloat16)
    out_ref[1] = z_score.T.astype(jnp.bfloat16)


def swap_kernel(in_ref, out_ref, held, send_sem, recv_sem):
    tile = lax.axis_index("tile")
    orient = lax.axis_index("orient")
    core = lax.rem(orient, 2)
    partner = (tile, (orient // 2) * 2 + 1 - core)
    barrier = pltpu.get_barrier_semaphore()
    pl.semaphore_signal(barrier, inc=1, device_id=partner, device_id_type=MESH)
    pl.semaphore_wait(barrier, 1)
    copy = pltpu.make_async_remote_copy(
        src_ref=in_ref, dst_ref=held, send_sem=send_sem, recv_sem=recv_sem,
        device_id=partner, device_id_type=MESH,
    )
    copy.start()
    for which in range(2):
        out_ref[which, core] = in_ref[which]
    copy.wait()
    for which in range(2):
        out_ref[which, 1 - core] = held[which]


def body(n_tile, n_orient, micrograph_tiles, tile_offsets, library, orient_ids):
    tile_count, length = micrograph_tiles.shape[:2]
    slots, _, size, _ = library.shape
    steps = orient_ids.shape[1]
    n_chip = n_orient // 2
    assert tile_count == 2 and n_orient % 2 == 0
    half = length // 2
    t = tables(length, VALID)
    rows = t["weight"].shape[0]
    f32, bf16 = jnp.float32, jnp.bfloat16
    shape = jax.ShapeDtypeStruct
    plane = shape((rows, length), f32)
    params = pltpu.CompilerParams(vmem_limit_bytes=GRANT)

    real, imag, contrast, power, picked = pl.pallas_call(
        forward_kernel,
        out_shape=(plane, plane, plane, shape((2, rows, half), bf16), shape((steps, size, size), bf16)),
        in_specs=[SMEM, SMEM] + [VMEM] * 7,
        out_specs=(VMEM,) * 5,
        compiler_params=params,
    )(
        orient_ids, tile_offsets, micrograph_tiles, library, t["first"], t["cos"], t["sin"],
        t["a_square"], t["b_square"],
    )

    copies = 3 + 2 * (n_tile - 1) + (n_chip - 1)
    total, templates = pl.pallas_call(
        functools.partial(exchange_kernel, n_tile, n_orient),
        out_shape=(shape((2, rows, half), f32), shape((2, n_chip, steps, size, size), bf16)),
        in_specs=[VMEM] * 2,
        out_specs=(VMEM,) * 2,
        scratch_shapes=[
            pltpu.VMEM((rows, half), bf16),
            pltpu.VMEM((rows, half), bf16),
            pltpu.VMEM((n_tile - 1, rows, half), bf16),
            pltpu.VMEM((rows, half), f32),
            pltpu.VMEM((rows, half), f32),
            pltpu.VMEM((n_tile - 1, steps, size, size), bf16),
            pltpu.VMEM((2, n_chip, steps, size, size), bf16),
            pltpu.SemaphoreType.DMA((copies,)),
            pltpu.SemaphoreType.DMA((copies,)),
        ],
        compiler_params=pltpu.CompilerParams(collective_id=0, has_side_effects=True),
    )(power, picked)

    found = pl.pallas_call(
        functools.partial(search_kernel, tile_count * n_tile),
        out_shape=shape((2, VALID, VALID), bf16),
        in_specs=[VMEM] * 12,
        out_specs=VMEM,
        scratch_shapes=[
            pltpu.VMEM((rows, length), f32),
            pltpu.VMEM((rows, length), f32),
            pltpu.VMEM((rows, length), f32),
            pltpu.VMEM((2 * size, 2 * length), bf16),
            pltpu.VMEM((length, steps * VALID), bf16),
            pltpu.VMEM((VALID, VALID), f32),
            pltpu.VMEM((VALID, VALID), f32),
            pltpu.VMEM((VALID, VALID), f32),
        ],
        compiler_params=params,
    )(
        real, imag, contrast, total, templates.reshape(n_orient, steps, size, size),
        np.ascontiguousarray(t["first"][:, :size]), t["cos"], t["sin"], t["even"], t["odd"],
        t["last"], t["weight"],
    )

    both = pl.pallas_call(
        swap_kernel,
        out_shape=shape((2, 2, VALID, VALID), bf16),
        in_specs=[VMEM],
        out_specs=VMEM,
        scratch_shapes=[
            pltpu.VMEM((2, VALID, VALID), bf16),
            pltpu.SemaphoreType.DMA,
            pltpu.SemaphoreType.DMA,
        ],
        compiler_params=pltpu.CompilerParams(collective_id=1, has_side_effects=True),
    )(found)
    return (both[0].astype(f32), both[1].astype(f32))


def solution(mesh):
    placed = (
        P("tile", None, None),
        P("tile", None),
        P("tile", "orient", None, None),
        P("orient", None),
    )
    return jax.shard_map(
        functools.partial(body, mesh.shape["tile"], mesh.shape["orient"]),
        mesh=mesh,
        in_specs=placed,
        out_specs=(P("tile", None, None), P("tile", None, None)),
        check_vma=False,
    )
```

```python
import functools
import math

import jax
import jax.numpy as jnp
import numpy as np
from jax import lax
from jax.experimental import pallas as pl
from jax.experimental.pallas import tpu as pltpu
from jax.sharding import PartitionSpec as P

VALID = 384

AMPLITUDE = 0.07
DEFOCUS_BASE = 100.0
DEFOCUS_TILT = 0.002
FLOOR_SHARE = 0.25
MESH = pl.DeviceIdType.MESH
VMEM = pl.BlockSpec(memory_space=pltpu.VMEM)
SMEM = pl.BlockSpec(memory_space=pltpu.SMEM)
GRANT = 56 * 1024 * 1024


def tables(length, valid):
    half = length // 2
    rows = -(-(half + 1) // 16) * 16
    a_index = np.concatenate([np.arange(0, length, 2), np.arange(1, length, 2)])
    j_index = np.arange(length)
    b_index = np.arange(half + 1)

    def wave(function, left, right):
        return function((left[:, None] * right[None, :]) % length * (2.0 * np.pi / length))

    first = np.zeros((2, rows, length))
    first[0, : half + 1] = wave(np.cos, b_index, j_index)
    first[1, : half + 1] = -wave(np.sin, b_index, j_index)
    second_cos = wave(np.cos, j_index, a_index)
    second_sin = wave(np.sin, j_index, a_index)
    back = []
    for parity in range(2):
        cosine = wave(np.cos, a_index[parity * half : (parity + 1) * half], j_index[:half])
        sine = wave(np.sin, a_index[parity * half : (parity + 1) * half], j_index[:half])
        back.append(np.block([[cosine, sine], [-sine, cosine]]))
    count = np.full((half,), 2.0)
    count[0] = 1.0
    last_cos = wave(np.cos, j_index[:valid], b_index[:half]) * count / length
    last_sin = -wave(np.sin, j_index[:valid], b_index[:half]) * count / length
    last_sin[:, 0] = np.cos(np.pi * j_index[:valid]) / length
    last = np.concatenate([last_cos, last_sin], axis=1)

    signed = np.where(a_index < half, a_index, a_index - length) / length
    a_square = (signed * signed)[None, :]
    b_square = np.zeros((rows, 1))
    b_square[: half + 1, 0] = (b_index / length) ** 2
    weight = np.zeros((rows, 1))
    weight[: half + 1, 0] = 2.0
    weight[0, 0] = weight[half, 0] = 1.0

    def narrow(value):
        return np.asarray(value, np.float32).astype(jnp.bfloat16)

    return dict(
        first=narrow(first.reshape(2 * rows, length)),
        cos=narrow(second_cos),
        sin=narrow(second_sin),
        even=narrow(back[0]),
        odd=narrow(back[1]),
        last=narrow(last),
        a_square=a_square.astype(np.float32),
        b_square=b_square.astype(np.float32),
        weight=weight.astype(np.float32),
    )


def dot(left, right):
    return jnp.dot(left, right, preferred_element_type=jnp.float32)


def dot_nt(left, right):
    return lax.dot_general(
        left, right, (((1,), (1,)), ((), ())), preferred_element_type=jnp.float32
    )


def sine_of_turns(turns):
    part = turns - jnp.floor(turns + 0.5)
    mirrored = jnp.where(part > 0.0, 0.5, -0.5) - part
    part = jnp.where(jnp.abs(part) > 0.25, mirrored, part)
    angle = part * (2.0 * math.pi)
    square = angle * angle
    poly = -1.0 / 39916800.0
    for term in (1.0 / 362880.0, -1.0 / 5040.0, 1.0 / 120.0, -1.0 / 6.0, 1.0):
        poly = poly * square + term
    return angle * poly


def opening_kernel(
    n_tile, n_orient,
    ids_ref, off_ref, x_ref, lib_ref, first_ref, cos_ref, sin_ref, a_ref, b_ref,
    real_ref, imag_ref, con_ref, total_ref, all_ref,
    power, pair_in, sum_out, sum_in, done_out, done_in, pick_out, pick_in, held,
    send_sem, recv_sem,
):
    tile = lax.axis_index("tile")
    orient = lax.axis_index("orient")
    core = lax.rem(orient, 2)
    chip = orient // 2
    n_chip = n_orient // 2
    bits = n_tile.bit_length() - 1
    rows, length = real_ref.shape
    half = length // 2
    slots = lib_ref.shape[0]
    steps = pick_out.shape[1]
    partner = (tile, chip * 2 + 1 - core)
    across = []
    for bit in range(bits):
        side = lax.rem(tile // (1 << bit), 2)
        across.append((tile + (1 - 2 * side) * (1 << bit), orient))
    chips = [(tile, lax.rem(chip + k, n_chip) * 2 + core) for k in range(1, n_chip)]

    barrier = pltpu.get_barrier_semaphore()
    for device in [partner] + across + chips:
        pl.semaphore_signal(barrier, inc=1, device_id=device, device_id_type=MESH)

    used = [0]

    def send(src, dst, device):
        at = used[0]
        used[0] += 1
        copy = pltpu.make_async_remote_copy(
            src_ref=src, dst_ref=dst, send_sem=send_sem.at[at], recv_sem=recv_sem.at[at],
            device_id=device, device_id_type=MESH,
        )
        copy.start()
        return copy

    for step in range(steps):
        chosen = ids_ref[0, step]
        owner = chosen // slots
        picked = lib_ref[chosen - owner * slots, 0]
        keep = jnp.where(owner == tile, 1.0, 0.0).astype(jnp.float32)
        pick_out[0, step] = jnp.where(keep > 0.0, picked.astype(jnp.float32), 0.0).astype(jnp.bfloat16)
    pl.semaphore_wait(barrier, 1 + len(across) + len(chips))

    def start_picks(stage):
        return [
            send(pick_out.at[stage, step], pick_in.at[stage, step], across[(stage + step) % bits])
            for step in range(steps)
        ]

    def end_picks(stage, copies):
        for step, copy in enumerate(copies):
            copy.wait()
            value = pick_out[stage, step].astype(jnp.float32) + pick_in[stage, step].astype(jnp.float32)
            if stage + 1 < bits:
                pick_out[stage + 1, step] = value.astype(jnp.bfloat16)
            else:
                held[core, chip, step] = value.astype(jnp.bfloat16)

    picks = start_picks(0)
    halves = dot_nt(first_ref[...], x_ref[core]).astype(jnp.bfloat16)
    half_real, half_imag = halves[:rows], halves[rows:]
    for stage in range(bits):
        end_picks(stage, picks)
        if stage + 1 < bits:
            picks = start_picks(stage + 1)
        if stage == 0:
            spec_real = dot(half_real, cos_ref[...]) + dot(half_imag, sin_ref[...])
    spread = [send(held.at[core, chip], held.at[core, chip], device) for device in chips]
    spec_imag = dot(half_imag, cos_ref[...]) - dot(half_real, sin_ref[...])
    value = spec_real * spec_real + spec_imag * spec_imag
    power[0] = value[:, :half].astype(jnp.bfloat16)
    power[1] = value[:, half:].astype(jnp.bfloat16)
    pair = send(power.at[1 - core], pair_in, partner)

    s2 = a_ref[...] + b_ref[...]
    tilt = (off_ref[core, 0] - off_ref[core, 1]).astype(jnp.float32)
    defocus = DEFOCUS_BASE + DEFOCUS_TILT * tilt
    shift = math.asin(AMPLITUDE) / (2.0 * math.pi)
    contrast = -sine_of_turns(s2 * (0.5 * defocus) + shift)
    contrast = jnp.where(s2 > 0.0, contrast, 0.0)
    con_ref[...] = contrast
    real_ref[...] = spec_real * contrast
    imag_ref[...] = spec_imag * contrast

    pair.wait()
    total = power[core].astype(jnp.float32) + pair_in[...].astype(jnp.float32)
    quarter = half // 2
    for stage in range(bits):
        sum_out[stage, 0] = total[:, :quarter].astype(jnp.bfloat16)
        sum_out[stage, 1] = total[:, quarter:].astype(jnp.bfloat16)
        copies = [
            send(sum_out.at[stage, piece], sum_in.at[stage, piece], across[(stage + piece) % bits])
            for piece in range(2)
        ]
        parts = []
        for piece, copy in enumerate(copies):
            copy.wait()
            parts.append(
                sum_out[stage, piece].astype(jnp.float32) + sum_in[stage, piece].astype(jnp.float32)
            )
        total = jnp.concatenate(parts, axis=1)
    done_out[...] = total
    last = send(done_out, done_in, partner)
    total_ref[core] = total
    for copy in spread:
        copy.wait()
    swap = send(held.at[core], held.at[core], partner)
    last.wait()
    total_ref[1 - core] = done_in[...]
    swap.wait()
    all_ref[...] = held[...]


def search_kernel(
    tiles, real_ref, imag_ref, con_ref, total_ref, tpl_ref, first_ref, cos_ref, sin_ref,
    even_ref, odd_ref, last_ref, weight_ref, out_ref,
    g_real, g_imag, g_energy, base_table, mids, peak, total_sum, squares,
):
    rows, length = real_ref.shape
    half = length // 2
    valid = last_ref.shape[0]
    groups, steps, size, _ = tpl_ref.shape
    weight = weight_ref[...]
    sides = [total_ref[side] / tiles for side in range(2)]
    mean = (jnp.sum(sides[0] * weight) + jnp.sum(sides[1] * weight)) / (length * length)
    floor = FLOOR_SHARE * mean
    for side in range(2):
        columns = slice(side * half, (side + 1) * half)
        whiten2 = 1.0 / jnp.maximum(sides[side], floor)
        contrast = con_ref[:, columns]
        g_real[:, columns] = real_ref[:, columns] * whiten2
        g_imag[:, columns] = imag_ref[:, columns] * whiten2
        g_energy[:, columns] = contrast * contrast * whiten2 * (weight / (length * length))
    base_table[:size, :length] = cos_ref[:size]
    base_table[:size, length:] = -sin_ref[:size]
    base_table[size:, :length] = sin_ref[:size]
    base_table[size:, length:] = cos_ref[:size]
    peak[...] = jnp.full_like(peak, -jnp.inf)
    total_sum[...] = jnp.zeros_like(total_sum)
    squares[...] = jnp.zeros_like(squares)

    def visit(group, carry):
        images = tpl_ref[group].reshape(steps * size, size)
        halves = dot_nt(first_ref[...], images).astype(jnp.bfloat16)
        scales = []
        for step in range(steps):
            columns = slice(step * size, (step + 1) * size)
            joined = jnp.concatenate([halves[:rows, columns], halves[rows:, columns]], axis=1)
            base = dot(joined, base_table[...])
            base_real, base_imag = base[:, :length], base[:, length:]
            energy = jnp.sum(g_energy[...] * (base_real * base_real + base_imag * base_imag))
            scales.append(lax.rsqrt(energy + 1e-06))
            prod_real = (g_real[...] * base_real + g_imag[...] * base_imag).astype(jnp.bfloat16)
            prod_imag = (g_imag[...] * base_real - g_real[...] * base_imag).astype(jnp.bfloat16)
            even = dot(
                jnp.concatenate([prod_real[:, :half], prod_imag[:, :half]], axis=1), even_ref[...]
            )
            odd = dot(
                jnp.concatenate([prod_real[:, half:], prod_imag[:, half:]], axis=1), odd_ref[...]
            )
            both, apart = even + odd, even - odd
            mid_real = jnp.concatenate([both[:, :half], apart[:, : valid - half]], axis=1)
            mid_imag = jnp.concatenate([both[:half, half:], apart[:half, half:valid]], axis=1)
            row = lax.broadcasted_iota(jnp.int32, (half, valid), 0)
            mid_imag = jnp.where(row == 0, mid_real[half : half + 1], mid_imag)
            place = slice(step * valid, (step + 1) * valid)
            mids[:half, place] = mid_real[:half].astype(jnp.bfloat16)
            mids[half:, place] = mid_imag.astype(jnp.bfloat16)
        found = dot(last_ref[...], mids[...])
        top, add, add2 = peak[...], total_sum[...], squares[...]
        for step in range(steps):
            score = found[:, step * valid : (step + 1) * valid] * scales[step]
            top = jnp.maximum(top, score)
            add = add + score
            add2 = add2 + score * score
        peak[...] = top
        total_sum[...] = add
        squares[...] = add2
        return carry

    lax.fori_loop(0, groups, visit, 0)
    searched = groups * steps
    mean_score = total_sum[...] / searched
    variance = squares[...] / searched - mean_score * mean_score
    z_score = (peak[...] - mean_score) * lax.rsqrt(variance + 1e-06)
    out_ref[0] = peak[...].T.astype(jnp.bfloat16)
    out_ref[1] = z_score.T.astype(jnp.bfloat16)


def swap_kernel(in_ref, out_ref, held, send_sem, recv_sem):
    tile = lax.axis_index("tile")
    orient = lax.axis_index("orient")
    core = lax.rem(orient, 2)
    partner = (tile, (orient // 2) * 2 + 1 - core)
    barrier = pltpu.get_barrier_semaphore()
    pl.semaphore_signal(barrier, inc=1, device_id=partner, device_id_type=MESH)
    pl.semaphore_wait(barrier, 1)
    copy = pltpu.make_async_remote_copy(
        src_ref=in_ref, dst_ref=held, send_sem=send_sem, recv_sem=recv_sem,
        device_id=partner, device_id_type=MESH,
    )
    copy.start()
    for which in range(2):
        out_ref[which, core] = in_ref[which]
    copy.wait()
    for which in range(2):
        out_ref[which, 1 - core] = held[which]


def body(n_tile, n_orient, micrograph_tiles, tile_offsets, library, orient_ids):
    tile_count, length = micrograph_tiles.shape[:2]
    slots, _, size, _ = library.shape
    steps = orient_ids.shape[1]
    n_chip = n_orient // 2
    assert tile_count == 2 and n_orient % 2 == 0 and n_tile & (n_tile - 1) == 0
    half = length // 2
    t = tables(length, VALID)
    rows = t["weight"].shape[0]
    f32, bf16 = jnp.float32, jnp.bfloat16
    shape = jax.ShapeDtypeStruct
    plane = shape((rows, length), f32)
    params = pltpu.CompilerParams(vmem_limit_bytes=GRANT)

    bits = n_tile.bit_length() - 1
    copies = 3 + bits * (steps + 2) + (n_chip - 1)
    real, imag, contrast, total, templates = pl.pallas_call(
        functools.partial(opening_kernel, n_tile, n_orient),
        out_shape=(
            plane, plane, plane, shape((2, rows, half), f32), shape((2, n_chip, steps, size, size), bf16)
        ),
        in_specs=[SMEM, SMEM] + [VMEM] * 7,
        out_specs=(VMEM,) * 5,
        scratch_shapes=[
            pltpu.VMEM((2, rows, half), bf16),
            pltpu.VMEM((rows, half), bf16),
            pltpu.VMEM((bits, 2, rows, half // 2), bf16),
            pltpu.VMEM((bits, 2, rows, half // 2), bf16),
            pltpu.VMEM((rows, half), f32),
            pltpu.VMEM((rows, half), f32),
            pltpu.VMEM((bits, steps, size, size), bf16),
            pltpu.VMEM((bits, steps, size, size), bf16),
            pltpu.VMEM((2, n_chip, steps, size, size), bf16),
            pltpu.SemaphoreType.DMA((copies,)),
            pltpu.SemaphoreType.DMA((copies,)),
        ],
        compiler_params=pltpu.CompilerParams(
            collective_id=0, has_side_effects=True, vmem_limit_bytes=GRANT
        ),
    )(
        orient_ids, tile_offsets, micrograph_tiles, library, t["first"], t["cos"], t["sin"],
        t["a_square"], t["b_square"],
    )

    found = pl.pallas_call(
        functools.partial(search_kernel, tile_count * n_tile),
        out_shape=shape((2, VALID, VALID), bf16),
        in_specs=[VMEM] * 12,
        out_specs=VMEM,
        scratch_shapes=[
            pltpu.VMEM((rows, length), f32),
            pltpu.VMEM((rows, length), f32),
            pltpu.VMEM((rows, length), f32),
            pltpu.VMEM((2 * size, 2 * length), bf16),
            pltpu.VMEM((length, steps * VALID), bf16),
            pltpu.VMEM((VALID, VALID), f32),
            pltpu.VMEM((VALID, VALID), f32),
            pltpu.VMEM((VALID, VALID), f32),
        ],
        compiler_params=params,
    )(
        real, imag, contrast, total, templates.reshape(n_orient, steps, size, size),
        np.ascontiguousarray(t["first"][:, :size]), t["cos"], t["sin"], t["even"], t["odd"],
        t["last"], t["weight"],
    )

    both = pl.pallas_call(
        swap_kernel,
        out_shape=shape((2, 2, VALID, VALID), bf16),
        in_specs=[VMEM],
        out_specs=VMEM,
        scratch_shapes=[
            pltpu.VMEM((2, VALID, VALID), bf16),
            pltpu.SemaphoreType.DMA,
            pltpu.SemaphoreType.DMA,
        ],
        compiler_params=pltpu.CompilerParams(collective_id=1, has_side_effects=True),
    )(found)
    return (both[0].astype(f32), both[1].astype(f32))


def solution(mesh):
    placed = (
        P("tile", None, None),
        P("tile", None),
        P("tile", "orient", None, None),
        P("orient", None),
    )
    return jax.shard_map(
        functools.partial(body, mesh.shape["tile"], mesh.shape["orient"]),
        mesh=mesh,
        in_specs=placed,
        out_specs=(P("tile", None, None), P("tile", None, None)),
        check_vma=False,
    )
```

```python
import functools
import math

import jax
import jax.numpy as jnp
import numpy as np
from jax import lax
from jax.experimental import pallas as pl
from jax.experimental.pallas import tpu as pltpu
from jax.sharding import PartitionSpec as P

VALID = 384

AMPLITUDE = 0.07
DEFOCUS_BASE = 100.0
DEFOCUS_TILT = 0.002
FLOOR_SHARE = 0.25
MESH = pl.DeviceIdType.MESH
VMEM = pl.BlockSpec(memory_space=pltpu.VMEM)
SMEM = pl.BlockSpec(memory_space=pltpu.SMEM)
GRANT = 56 * 1024 * 1024


def tables(length, valid):
    half = length // 2
    rows = -(-(half + 1) // 16) * 16
    a_index = np.concatenate([np.arange(0, length, 2), np.arange(1, length, 2)])
    j_index = np.arange(length)
    b_index = np.arange(half + 1)

    def wave(function, left, right):
        return function((left[:, None] * right[None, :]) % length * (2.0 * np.pi / length))

    first = np.zeros((2, rows, length))
    first[0, : half + 1] = wave(np.cos, b_index, j_index)
    first[1, : half + 1] = -wave(np.sin, b_index, j_index)
    second_cos = wave(np.cos, j_index, a_index)
    second_sin = wave(np.sin, j_index, a_index)
    back = []
    for parity in range(2):
        cosine = wave(np.cos, a_index[parity * half : (parity + 1) * half], j_index[:half])
        sine = wave(np.sin, a_index[parity * half : (parity + 1) * half], j_index[:half])
        back.append(np.block([[cosine, sine], [-sine, cosine]]))
    count = np.full((half,), 2.0)
    count[0] = 1.0
    last_cos = wave(np.cos, j_index[:valid], b_index[:half]) * count / length
    last_sin = -wave(np.sin, j_index[:valid], b_index[:half]) * count / length
    last_sin[:, 0] = np.cos(np.pi * j_index[:valid]) / length
    last = np.concatenate([last_cos, last_sin], axis=1)

    signed = np.where(a_index < half, a_index, a_index - length) / length
    a_square = (signed * signed)[None, :]
    b_square = np.zeros((rows, 1))
    b_square[: half + 1, 0] = (b_index / length) ** 2
    weight = np.zeros((rows, 1))
    weight[: half + 1, 0] = 2.0
    weight[0, 0] = weight[half, 0] = 1.0

    def narrow(value):
        return np.asarray(value, np.float32).astype(jnp.bfloat16)

    return dict(
        first=narrow(first.reshape(2 * rows, length)),
        cos=narrow(second_cos),
        sin=narrow(second_sin),
        even=narrow(back[0]),
        odd=narrow(back[1]),
        last=narrow(last),
        a_square=a_square.astype(np.float32),
        b_square=b_square.astype(np.float32),
        weight=weight.astype(np.float32),
    )


def dot(left, right):
    return jnp.dot(left, right, preferred_element_type=jnp.float32)


def dot_nt(left, right):
    return lax.dot_general(
        left, right, (((1,), (1,)), ((), ())), preferred_element_type=jnp.float32
    )


def sine_of_turns(turns):
    part = turns - jnp.floor(turns + 0.5)
    mirrored = jnp.where(part > 0.0, 0.5, -0.5) - part
    part = jnp.where(jnp.abs(part) > 0.25, mirrored, part)
    angle = part * (2.0 * math.pi)
    square = angle * angle
    poly = -1.0 / 39916800.0
    for term in (1.0 / 362880.0, -1.0 / 5040.0, 1.0 / 120.0, -1.0 / 6.0, 1.0):
        poly = poly * square + term
    return angle * poly


def forward_kernel(
    ids_ref, off_ref, x_ref, lib_ref, first_ref, cos_ref, sin_ref, a_ref, b_ref,
    real_ref, imag_ref, con_ref, pow_ref, tpl_ref,
):
    core = lax.rem(lax.axis_index("orient"), 2)
    mine = lax.axis_index("tile")
    slots = lib_ref.shape[0]
    rows, length = real_ref.shape
    half = length // 2
    for step in range(tpl_ref.shape[0]):
        chosen = ids_ref[0, step]
        owner = chosen // slots
        picked = lib_ref[chosen - owner * slots, 0]
        keep = jnp.where(owner == mine, 1.0, 0.0).astype(jnp.float32)
        tpl_ref[step] = jnp.where(keep > 0.0, picked.astype(jnp.float32), 0.0).astype(jnp.bfloat16)
    halves = dot_nt(first_ref[...], x_ref[core]).astype(jnp.bfloat16)
    half_real, half_imag = halves[:rows], halves[rows:]
    spec_real = dot(half_real, cos_ref[...]) + dot(half_imag, sin_ref[...])
    spec_imag = dot(half_imag, cos_ref[...]) - dot(half_real, sin_ref[...])
    power = spec_real * spec_real + spec_imag * spec_imag
    pow_ref[0] = power[:, :half].astype(jnp.bfloat16)
    pow_ref[1] = power[:, half:].astype(jnp.bfloat16)
    s2 = a_ref[...] + b_ref[...]
    tilt = (off_ref[core, 0] - off_ref[core, 1]).astype(jnp.float32)
    defocus = DEFOCUS_BASE + DEFOCUS_TILT * tilt
    shift = math.asin(AMPLITUDE) / (2.0 * math.pi)
    contrast = -sine_of_turns(s2 * (0.5 * defocus) + shift)
    contrast = jnp.where(s2 > 0.0, contrast, 0.0)
    con_ref[...] = contrast
    real_ref[...] = spec_real * contrast
    imag_ref[...] = spec_imag * contrast


def exchange_kernel(
    n_tile, n_orient, pow_ref, tpl_ref, total_ref, all_ref,
    pair_in, half_out, half_in, done_out, done_in, tpl_in, held, send_sem, recv_sem,
):
    tile = lax.axis_index("tile")
    orient = lax.axis_index("orient")
    core = lax.rem(orient, 2)
    chip = orient // 2
    n_chip = n_orient // 2
    partner = (tile, chip * 2 + 1 - core)
    tiles = [(lax.rem(tile + k, n_tile), orient) for k in range(1, n_tile)]
    chips = [(tile, lax.rem(chip + k, n_chip) * 2 + core) for k in range(1, n_chip)]

    barrier = pltpu.get_barrier_semaphore()
    for device in [partner] + tiles + chips:
        pl.semaphore_signal(barrier, inc=1, device_id=device, device_id_type=MESH)
    pl.semaphore_wait(barrier, 1 + len(tiles) + len(chips))

    used = [0]

    def send(src, dst, device):
        at = used[0]
        used[0] += 1
        copy = pltpu.make_async_remote_copy(
            src_ref=src, dst_ref=dst, send_sem=send_sem.at[at], recv_sem=recv_sem.at[at],
            device_id=device, device_id_type=MESH,
        )
        copy.start()
        return copy

    pair = send(pow_ref.at[1 - core], pair_in, partner)
    picks = [send(tpl_ref, tpl_in.at[k], device) for k, device in enumerate(tiles)]
    pair.wait()
    mine = pow_ref[core].astype(jnp.float32) + pair_in[...].astype(jnp.float32)
    half_out[...] = mine.astype(jnp.bfloat16)
    sums = [send(half_out, half_in.at[k], device) for k, device in enumerate(tiles)]
    template = tpl_ref[...].astype(jnp.float32)
    for k, copy in enumerate(picks):
        copy.wait()
        template = template + tpl_in[k].astype(jnp.float32)
    held[core, chip] = template.astype(jnp.bfloat16)
    spread = [send(held.at[core, chip], held.at[core, chip], device) for device in chips]
    for copy in sums:
        copy.wait()
    total = half_out[...].astype(jnp.float32)
    for k in range(len(tiles)):
        total = total + half_in[k].astype(jnp.float32)
    done_out[...] = total
    last = send(done_out, done_in, partner)
    for copy in spread:
        copy.wait()
    swap = send(held.at[core], held.at[core], partner)
    total_ref[core] = total
    last.wait()
    total_ref[1 - core] = done_in[...]
    swap.wait()
    all_ref[...] = held[...]


def search_kernel(
    tiles, real_ref, imag_ref, con_ref, total_ref, tpl_ref, first_ref, cos_ref, sin_ref,
    even_ref, odd_ref, last_ref, weight_ref, out_ref,
    g_real, g_imag, g_energy, base_table, mids, peak, total_sum, squares,
):
    rows, length = real_ref.shape
    half = length // 2
    valid = last_ref.shape[0]
    groups, steps, size, _ = tpl_ref.shape
    weight = weight_ref[...]
    sides = [total_ref[side] / tiles for side in range(2)]
    mean = (jnp.sum(sides[0] * weight) + jnp.sum(sides[1] * weight)) / (length * length)
    floor = FLOOR_SHARE * mean
    for side in range(2):
        columns = slice(side * half, (side + 1) * half)
        whiten2 = 1.0 / jnp.maximum(sides[side], floor)
        contrast = con_ref[:, columns]
        g_real[:, columns] = (real_ref[:, columns] * whiten2).astype(jnp.bfloat16)
        g_imag[:, columns] = (imag_ref[:, columns] * whiten2).astype(jnp.bfloat16)
        g_energy[:, columns] = contrast * contrast * whiten2 * (weight / (length * length))
    base_table[:size, :length] = cos_ref[:size]
    base_table[:size, length:] = -sin_ref[:size]
    base_table[size:, :length] = sin_ref[:size]
    base_table[size:, length:] = cos_ref[:size]
    peak[...] = jnp.full_like(peak, -jnp.inf)
    total_sum[...] = jnp.zeros_like(total_sum)
    squares[...] = jnp.zeros_like(squares)

    def visit(group, carry):
        images = tpl_ref[group].reshape(steps * size, size)
        halves = dot_nt(first_ref[...], images).astype(jnp.bfloat16)
        scales = []
        for step in range(steps):
            columns = slice(step * size, (step + 1) * size)
            joined = jnp.concatenate([halves[:rows, columns], halves[rows:, columns]], axis=1)
            base = dot(joined, base_table[...])
            base_real, base_imag = base[:, :length], base[:, length:]
            energy = jnp.sum(g_energy[...] * (base_real * base_real + base_imag * base_imag))
            scales.append(lax.rsqrt(energy + 1e-06))
            short_real, short_imag = base_real.astype(jnp.bfloat16), base_imag.astype(jnp.bfloat16)
            prod_real = g_real[...] * short_real + g_imag[...] * short_imag
            prod_imag = g_imag[...] * short_real - g_real[...] * short_imag
            even = dot(
                jnp.concatenate([prod_real[:, :half], prod_imag[:, :half]], axis=1), even_ref[...]
            )
            odd = dot(
                jnp.concatenate([prod_real[:, half:], prod_imag[:, half:]], axis=1), odd_ref[...]
            )
            both, apart = even + odd, even - odd
            mid_real = jnp.concatenate([both[:, :half], apart[:, : valid - half]], axis=1)
            mid_imag = jnp.concatenate([both[:half, half:], apart[:half, half:valid]], axis=1)
            row = lax.broadcasted_iota(jnp.int32, (half, valid), 0)
            mid_imag = jnp.where(row == 0, mid_real[half : half + 1], mid_imag)
            place = slice(step * valid, (step + 1) * valid)
            mids[:half, place] = mid_real[:half].astype(jnp.bfloat16)
            mids[half:, place] = mid_imag.astype(jnp.bfloat16)
        found = dot(last_ref[...], mids[...])
        top, add, add2 = peak[...], total_sum[...], squares[...]
        for step in range(steps):
            score = found[:, step * valid : (step + 1) * valid] * scales[step]
            top = jnp.maximum(top, score)
            add = add + score
            add2 = add2 + score * score
        peak[...] = top
        total_sum[...] = add
        squares[...] = add2
        return carry

    lax.fori_loop(0, groups, visit, 0)
    searched = groups * steps
    mean_score = total_sum[...] / searched
    variance = squares[...] / searched - mean_score * mean_score
    z_score = (peak[...] - mean_score) * lax.rsqrt(variance + 1e-06)
    out_ref[0] = peak[...].T.astype(jnp.bfloat16)
    out_ref[1] = z_score.T.astype(jnp.bfloat16)


def swap_kernel(in_ref, out_ref, held, send_sem, recv_sem):
    tile = lax.axis_index("tile")
    orient = lax.axis_index("orient")
    core = lax.rem(orient, 2)
    partner = (tile, (orient // 2) * 2 + 1 - core)
    barrier = pltpu.get_barrier_semaphore()
    pl.semaphore_signal(barrier, inc=1, device_id=partner, device_id_type=MESH)
    pl.semaphore_wait(barrier, 1)
    copy = pltpu.make_async_remote_copy(
        src_ref=in_ref, dst_ref=held, send_sem=send_sem, recv_sem=recv_sem,
        device_id=partner, device_id_type=MESH,
    )
    copy.start()
    for which in range(2):
        out_ref[which, core] = in_ref[which]
    copy.wait()
    for which in range(2):
        out_ref[which, 1 - core] = held[which]


def body(n_tile, n_orient, micrograph_tiles, tile_offsets, library, orient_ids):
    tile_count, length = micrograph_tiles.shape[:2]
    slots, _, size, _ = library.shape
    steps = orient_ids.shape[1]
    n_chip = n_orient // 2
    assert tile_count == 2 and n_orient % 2 == 0
    half = length // 2
    t = tables(length, VALID)
    rows = t["weight"].shape[0]
    f32, bf16 = jnp.float32, jnp.bfloat16
    shape = jax.ShapeDtypeStruct
    plane = shape((rows, length), f32)
    params = pltpu.CompilerParams(vmem_limit_bytes=GRANT)

    real, imag, contrast, power, picked = pl.pallas_call(
        forward_kernel,
        out_shape=(plane, plane, plane, shape((2, rows, half), bf16), shape((steps, size, size), bf16)),
        in_specs=[SMEM, SMEM] + [VMEM] * 7,
        out_specs=(VMEM,) * 5,
        compiler_params=params,
    )(
        orient_ids, tile_offsets, micrograph_tiles, library, t["first"], t["cos"], t["sin"],
        t["a_square"], t["b_square"],
    )

    copies = 3 + 2 * (n_tile - 1) + (n_chip - 1)
    total, templates = pl.pallas_call(
        functools.partial(exchange_kernel, n_tile, n_orient),
        out_shape=(shape((2, rows, half), f32), shape((2, n_chip, steps, size, size), bf16)),
        in_specs=[VMEM] * 2,
        out_specs=(VMEM,) * 2,
        scratch_shapes=[
            pltpu.VMEM((rows, half), bf16),
            pltpu.VMEM((rows, half), bf16),
            pltpu.VMEM((n_tile - 1, rows, half), bf16),
            pltpu.VMEM((rows, half), f32),
            pltpu.VMEM((rows, half), f32),
            pltpu.VMEM((n_tile - 1, steps, size, size), bf16),
            pltpu.VMEM((2, n_chip, steps, size, size), bf16),
            pltpu.SemaphoreType.DMA((copies,)),
            pltpu.SemaphoreType.DMA((copies,)),
        ],
        compiler_params=pltpu.CompilerParams(collective_id=0, has_side_effects=True),
    )(power, picked)

    found = pl.pallas_call(
        functools.partial(search_kernel, tile_count * n_tile),
        out_shape=shape((2, VALID, VALID), bf16),
        in_specs=[VMEM] * 12,
        out_specs=VMEM,
        scratch_shapes=[
            pltpu.VMEM((rows, length), bf16),
            pltpu.VMEM((rows, length), bf16),
            pltpu.VMEM((rows, length), f32),
            pltpu.VMEM((2 * size, 2 * length), bf16),
            pltpu.VMEM((length, steps * VALID), bf16),
            pltpu.VMEM((VALID, VALID), f32),
            pltpu.VMEM((VALID, VALID), f32),
            pltpu.VMEM((VALID, VALID), f32),
        ],
        compiler_params=params,
    )(
        real, imag, contrast, total, templates.reshape(n_orient, steps, size, size),
        np.ascontiguousarray(t["first"][:, :size]), t["cos"], t["sin"], t["even"], t["odd"],
        t["last"], t["weight"],
    )

    both = pl.pallas_call(
        swap_kernel,
        out_shape=shape((2, 2, VALID, VALID), bf16),
        in_specs=[VMEM],
        out_specs=VMEM,
        scratch_shapes=[
            pltpu.VMEM((2, VALID, VALID), bf16),
            pltpu.SemaphoreType.DMA,
            pltpu.SemaphoreType.DMA,
        ],
        compiler_params=pltpu.CompilerParams(collective_id=1, has_side_effects=True),
    )(found)
    return (both[0].astype(f32), both[1].astype(f32))


def solution(mesh):
    placed = (
        P("tile", None, None),
        P("tile", None),
        P("tile", "orient", None, None),
        P("orient", None),
    )
    return jax.shard_map(
        functools.partial(body, mesh.shape["tile"], mesh.shape["orient"]),
        mesh=mesh,
        in_specs=placed,
        out_specs=(P("tile", None, None), P("tile", None, None)),
        check_vma=False,
    )
```

```python
import functools
import math

import jax
import jax.numpy as jnp
import numpy as np
from jax import lax
from jax.experimental import pallas as pl
from jax.experimental.pallas import tpu as pltpu
from jax.sharding import PartitionSpec as P

VALID = 384

AMPLITUDE = 0.07
DEFOCUS_BASE = 100.0
DEFOCUS_TILT = 0.002
FLOOR_SHARE = 0.25
MESH = pl.DeviceIdType.MESH
VMEM = pl.BlockSpec(memory_space=pltpu.VMEM)
SMEM = pl.BlockSpec(memory_space=pltpu.SMEM)
GRANT = 56 * 1024 * 1024


def tables(length, valid):
    half = length // 2
    rows = -(-(half + 1) // 16) * 16
    a_index = np.concatenate([np.arange(0, length, 2), np.arange(1, length, 2)])
    j_index = np.arange(length)
    b_index = np.arange(half + 1)

    def wave(function, left, right):
        return function((left[:, None] * right[None, :]) % length * (2.0 * np.pi / length))

    first = np.zeros((2, rows, length))
    first[0, : half + 1] = wave(np.cos, b_index, j_index)
    first[1, : half + 1] = -wave(np.sin, b_index, j_index)
    second_cos = wave(np.cos, j_index, a_index)
    second_sin = wave(np.sin, j_index, a_index)
    back = []
    for parity in range(2):
        cosine = wave(np.cos, a_index[parity * half : (parity + 1) * half], j_index[:half])
        sine = wave(np.sin, a_index[parity * half : (parity + 1) * half], j_index[:half])
        back.append(np.block([[cosine, sine], [-sine, cosine]]))
    count = np.full((half,), 2.0)
    count[0] = 1.0
    last_cos = wave(np.cos, j_index[:valid], b_index[:half]) * count / length
    last_sin = -wave(np.sin, j_index[:valid], b_index[:half]) * count / length
    last_sin[:, 0] = np.cos(np.pi * j_index[:valid]) / length
    last = np.concatenate([last_cos, last_sin], axis=1)

    signed = np.where(a_index < half, a_index, a_index - length) / length
    a_square = (signed * signed)[None, :]
    b_square = np.zeros((rows, 1))
    b_square[: half + 1, 0] = (b_index / length) ** 2
    weight = np.zeros((rows, 1))
    weight[: half + 1, 0] = 2.0
    weight[0, 0] = weight[half, 0] = 1.0

    def narrow(value):
        return np.asarray(value, np.float32).astype(jnp.bfloat16)

    return dict(
        first=narrow(first.reshape(2 * rows, length)),
        cos=narrow(second_cos),
        sin=narrow(second_sin),
        even=narrow(back[0]),
        odd=narrow(back[1]),
        last=narrow(last),
        a_square=a_square.astype(np.float32),
        b_square=b_square.astype(np.float32),
        weight=weight.astype(np.float32),
    )


def dot(left, right):
    return jnp.dot(left, right, preferred_element_type=jnp.float32)


def dot_nt(left, right):
    return lax.dot_general(
        left, right, (((1,), (1,)), ((), ())), preferred_element_type=jnp.float32
    )


def sine_of_turns(turns):
    part = turns - jnp.floor(turns + 0.5)
    mirrored = jnp.where(part > 0.0, 0.5, -0.5) - part
    part = jnp.where(jnp.abs(part) > 0.25, mirrored, part)
    angle = part * (2.0 * math.pi)
    square = angle * angle
    poly = -1.0 / 39916800.0
    for term in (1.0 / 362880.0, -1.0 / 5040.0, 1.0 / 120.0, -1.0 / 6.0, 1.0):
        poly = poly * square + term
    return angle * poly


def forward_kernel(
    ids_ref, off_ref, x_ref, lib_ref, first_ref, cos_ref, sin_ref, a_ref, b_ref,
    real_ref, imag_ref, con_ref, pow_ref, tpl_ref,
):
    core = lax.rem(lax.axis_index("orient"), 2)
    mine = lax.axis_index("tile")
    slots = lib_ref.shape[0]
    rows, length = real_ref.shape
    half = length // 2
    for step in range(tpl_ref.shape[0]):
        chosen = ids_ref[0, step]
        owner = chosen // slots
        picked = lib_ref[chosen - owner * slots, 0]
        keep = jnp.where(owner == mine, 1.0, 0.0).astype(jnp.float32)
        tpl_ref[step] = jnp.where(keep > 0.0, picked.astype(jnp.float32), 0.0).astype(jnp.bfloat16)
    halves = dot_nt(first_ref[...], x_ref[core]).astype(jnp.bfloat16)
    half_real, half_imag = halves[:rows], halves[rows:]
    spec_real = dot(half_real, cos_ref[...]) + dot(half_imag, sin_ref[...])
    spec_imag = dot(half_imag, cos_ref[...]) - dot(half_real, sin_ref[...])
    power = spec_real * spec_real + spec_imag * spec_imag
    pow_ref[0] = power[:, :half].astype(jnp.bfloat16)
    pow_ref[1] = power[:, half:].astype(jnp.bfloat16)
    s2 = a_ref[...] + b_ref[...]
    tilt = (off_ref[core, 0] - off_ref[core, 1]).astype(jnp.float32)
    defocus = DEFOCUS_BASE + DEFOCUS_TILT * tilt
    shift = math.asin(AMPLITUDE) / (2.0 * math.pi)
    contrast = -sine_of_turns(s2 * (0.5 * defocus) + shift)
    contrast = jnp.where(s2 > 0.0, contrast, 0.0)
    con_ref[...] = contrast
    real_ref[...] = spec_real * contrast
    imag_ref[...] = spec_imag * contrast


def exchange_kernel(
    n_tile, n_orient, pow_ref, tpl_ref, total_ref, all_ref,
    pair_in, half_out, half_in, done_out, done_in, tpl_in, held, send_sem, recv_sem,
):
    tile = lax.axis_index("tile")
    orient = lax.axis_index("orient")
    core = lax.rem(orient, 2)
    chip = orient // 2
    n_chip = n_orient // 2
    partner = (tile, chip * 2 + 1 - core)
    tiles = [(lax.rem(tile + k, n_tile), orient) for k in range(1, n_tile)]
    chips = [(tile, lax.rem(chip + k, n_chip) * 2 + core) for k in range(1, n_chip)]

    barrier = pltpu.get_barrier_semaphore()
    for device in [partner] + tiles + chips:
        pl.semaphore_signal(barrier, inc=1, device_id=device, device_id_type=MESH)
    pl.semaphore_wait(barrier, 1 + len(tiles) + len(chips))

    used = [0]

    def send(src, dst, device):
        at = used[0]
        used[0] += 1
        copy = pltpu.make_async_remote_copy(
            src_ref=src, dst_ref=dst, send_sem=send_sem.at[at], recv_sem=recv_sem.at[at],
            device_id=device, device_id_type=MESH,
        )
        copy.start()
        return copy

    pair = send(pow_ref.at[1 - core], pair_in, partner)
    picks = [send(tpl_ref, tpl_in.at[k], device) for k, device in enumerate(tiles)]
    pair.wait()
    mine = pow_ref[core].astype(jnp.float32) + pair_in[...].astype(jnp.float32)
    half_out[...] = mine.astype(jnp.bfloat16)
    sums = [send(half_out, half_in.at[k], device) for k, device in enumerate(tiles)]
    template = tpl_ref[...].astype(jnp.float32)
    for k, copy in enumerate(picks):
        copy.wait()
        template = template + tpl_in[k].astype(jnp.float32)
    held[core, chip] = template.astype(jnp.bfloat16)
    spread = [send(held.at[core, chip], held.at[core, chip], device) for device in chips]
    for copy in sums:
        copy.wait()
    total = half_out[...].astype(jnp.float32)
    for k in range(len(tiles)):
        total = total + half_in[k].astype(jnp.float32)
    done_out[...] = total
    last = send(done_out, done_in, partner)
    for copy in spread:
        copy.wait()
    swap = send(held.at[core], held.at[core], partner)
    total_ref[core] = total
    last.wait()
    total_ref[1 - core] = done_in[...]
    swap.wait()
    all_ref[...] = held[...]


def search_kernel(
    tiles, real_ref, imag_ref, con_ref, total_ref, tpl_ref, first_ref, cos_ref, sin_ref,
    even_ref, odd_ref, last_ref, weight_ref, out_ref, peak_ref, z_ref,
    wide, copy_sem, g_real, g_imag, g_energy, base_table, mids, peak, total_sum, squares,
):
    rows, length = real_ref.shape
    half = length // 2
    valid = last_ref.shape[0]
    groups, steps, size, _ = tpl_ref.shape
    weight = weight_ref[...]
    sides = [total_ref[side] / tiles for side in range(2)]
    mean = (jnp.sum(sides[0] * weight) + jnp.sum(sides[1] * weight)) / (length * length)
    floor = FLOOR_SHARE * mean
    for side in range(2):
        columns = slice(side * half, (side + 1) * half)
        whiten2 = 1.0 / jnp.maximum(sides[side], floor)
        contrast = con_ref[:, columns]
        g_real[:, columns] = (real_ref[:, columns] * whiten2).astype(jnp.bfloat16)
        g_imag[:, columns] = (imag_ref[:, columns] * whiten2).astype(jnp.bfloat16)
        g_energy[:, columns] = contrast * contrast * whiten2 * (weight / (length * length))
    base_table[:size, :length] = cos_ref[:size]
    base_table[:size, length:] = -sin_ref[:size]
    base_table[size:, :length] = sin_ref[:size]
    base_table[size:, length:] = cos_ref[:size]
    peak[...] = jnp.full_like(peak, -jnp.inf)
    total_sum[...] = jnp.zeros_like(total_sum)
    squares[...] = jnp.zeros_like(squares)

    def visit(group, carry):
        images = tpl_ref[group].reshape(steps * size, size)
        halves = dot_nt(first_ref[...], images).astype(jnp.bfloat16)
        scales = []
        for step in range(steps):
            columns = slice(step * size, (step + 1) * size)
            joined = jnp.concatenate([halves[:rows, columns], halves[rows:, columns]], axis=1)
            base = dot(joined, base_table[...])
            base_real, base_imag = base[:, :length], base[:, length:]
            energy = jnp.sum(g_energy[...] * (base_real * base_real + base_imag * base_imag))
            scales.append(lax.rsqrt(energy + 1e-06))
            short_real, short_imag = base_real.astype(jnp.bfloat16), base_imag.astype(jnp.bfloat16)
            prod_real = g_real[...] * short_real + g_imag[...] * short_imag
            prod_imag = g_imag[...] * short_real - g_real[...] * short_imag
            even = dot(
                jnp.concatenate([prod_real[:, :half], prod_imag[:, :half]], axis=1), even_ref[...]
            )
            odd = dot(
                jnp.concatenate([prod_real[:, half:], prod_imag[:, half:]], axis=1), odd_ref[...]
            )
            both, apart = even + odd, even - odd
            mid_real = jnp.concatenate([both[:, :half], apart[:, : valid - half]], axis=1)
            mid_imag = jnp.concatenate([both[:half, half:], apart[:half, half:valid]], axis=1)
            row = lax.broadcasted_iota(jnp.int32, (half, valid), 0)
            mid_imag = jnp.where(row == 0, mid_real[half : half + 1], mid_imag)
            place = slice(step * valid, (step + 1) * valid)
            mids[:half, place] = mid_real[:half].astype(jnp.bfloat16)
            mids[half:, place] = mid_imag.astype(jnp.bfloat16)
        found = dot(last_ref[...], mids[...])
        top, add, add2 = peak[...], total_sum[...], squares[...]
        for step in range(steps):
            score = found[:, step * valid : (step + 1) * valid] * scales[step]
            top = jnp.maximum(top, score)
            add = add + score
            add2 = add2 + score * score
        peak[...] = top
        total_sum[...] = add
        squares[...] = add2
        return carry

    lax.fori_loop(0, groups, visit, 0)
    searched = groups * steps
    mean_score = total_sum[...] / searched
    variance = squares[...] / searched - mean_score * mean_score
    z_score = (peak[...] - mean_score) * lax.rsqrt(variance + 1e-06)
    core = lax.rem(lax.axis_index("orient"), 2)
    copies = []
    for which, (value, place) in enumerate(((peak[...], peak_ref), (z_score, z_ref))):
        short = value.T.astype(jnp.bfloat16)
        out_ref[which] = short
        wide[which] = short.astype(jnp.float32)
        copy = pltpu.make_async_copy(wide.at[which], place.at[core], copy_sem.at[which])
        copy.start()
        copies.append(copy)
    for copy in copies:
        copy.wait()


def swap_kernel(in_ref, out_ref, held, send_sem, recv_sem):
    tile = lax.axis_index("tile")
    orient = lax.axis_index("orient")
    core = lax.rem(orient, 2)
    partner = (tile, (orient // 2) * 2 + 1 - core)
    barrier = pltpu.get_barrier_semaphore()
    pl.semaphore_signal(barrier, inc=1, device_id=partner, device_id_type=MESH)
    pl.semaphore_wait(barrier, 1)
    copy = pltpu.make_async_remote_copy(
        src_ref=in_ref, dst_ref=held, send_sem=send_sem, recv_sem=recv_sem,
        device_id=partner, device_id_type=MESH,
    )
    copy.start()
    copy.wait()
    out_ref[...] = held[...]


def body(n_tile, n_orient, micrograph_tiles, tile_offsets, library, orient_ids):
    tile_count, length = micrograph_tiles.shape[:2]
    slots, _, size, _ = library.shape
    steps = orient_ids.shape[1]
    n_chip = n_orient // 2
    assert tile_count == 2 and n_orient % 2 == 0
    half = length // 2
    t = tables(length, VALID)
    rows = t["weight"].shape[0]
    f32, bf16 = jnp.float32, jnp.bfloat16
    shape = jax.ShapeDtypeStruct
    plane = shape((rows, length), f32)
    params = pltpu.CompilerParams(vmem_limit_bytes=GRANT)

    real, imag, contrast, power, picked = pl.pallas_call(
        forward_kernel,
        out_shape=(plane, plane, plane, shape((2, rows, half), bf16), shape((steps, size, size), bf16)),
        in_specs=[SMEM, SMEM] + [VMEM] * 7,
        out_specs=(VMEM,) * 5,
        compiler_params=params,
    )(
        orient_ids, tile_offsets, micrograph_tiles, library, t["first"], t["cos"], t["sin"],
        t["a_square"], t["b_square"],
    )

    copies = 3 + 2 * (n_tile - 1) + (n_chip - 1)
    total, templates = pl.pallas_call(
        functools.partial(exchange_kernel, n_tile, n_orient),
        out_shape=(shape((2, rows, half), f32), shape((2, n_chip, steps, size, size), bf16)),
        in_specs=[VMEM] * 2,
        out_specs=(VMEM,) * 2,
        scratch_shapes=[
            pltpu.VMEM((rows, half), bf16),
            pltpu.VMEM((rows, half), bf16),
            pltpu.VMEM((n_tile - 1, rows, half), bf16),
            pltpu.VMEM((rows, half), f32),
            pltpu.VMEM((rows, half), f32),
            pltpu.VMEM((n_tile - 1, steps, size, size), bf16),
            pltpu.VMEM((2, n_chip, steps, size, size), bf16),
            pltpu.SemaphoreType.DMA((copies,)),
            pltpu.SemaphoreType.DMA((copies,)),
        ],
        compiler_params=pltpu.CompilerParams(collective_id=0, has_side_effects=True),
    )(power, picked)

    found, peak, z_score = pl.pallas_call(
        functools.partial(search_kernel, tile_count * n_tile),
        out_shape=(shape((2, VALID, VALID), bf16),) + (shape((2, VALID, VALID), f32),) * 2,
        in_specs=[VMEM] * 12,
        out_specs=(VMEM, pl.BlockSpec(memory_space=pl.ANY), pl.BlockSpec(memory_space=pl.ANY)),
        scratch_shapes=[
            pltpu.VMEM((2, VALID, VALID), f32),
            pltpu.SemaphoreType.DMA((2,)),
            pltpu.VMEM((rows, length), bf16),
            pltpu.VMEM((rows, length), bf16),
            pltpu.VMEM((rows, length), f32),
            pltpu.VMEM((2 * size, 2 * length), bf16),
            pltpu.VMEM((length, steps * VALID), bf16),
            pltpu.VMEM((VALID, VALID), f32),
            pltpu.VMEM((VALID, VALID), f32),
            pltpu.VMEM((VALID, VALID), f32),
        ],
        compiler_params=params,
    )(
        real, imag, contrast, total, templates.reshape(n_orient, steps, size, size),
        np.ascontiguousarray(t["first"][:, :size]), t["cos"], t["sin"], t["even"], t["odd"],
        t["last"], t["weight"],
    )

    other = pl.pallas_call(
        swap_kernel,
        out_shape=shape((2, VALID, VALID), bf16),
        in_specs=[VMEM],
        out_specs=VMEM,
        scratch_shapes=[
            pltpu.VMEM((2, VALID, VALID), bf16),
            pltpu.SemaphoreType.DMA,
            pltpu.SemaphoreType.DMA,
        ],
        compiler_params=pltpu.CompilerParams(collective_id=1, has_side_effects=True),
    )(found)
    place = 1 - lax.axis_index("orient") % 2
    return tuple(
        lax.dynamic_update_index_in_dim(whole, other[which].astype(f32), place, 0)
        for which, whole in enumerate((peak, z_score))
    )


def solution(mesh):
    placed = (
        P("tile", None, None),
        P("tile", None),
        P("tile", "orient", None, None),
        P("orient", None),
    )
    return jax.shard_map(
        functools.partial(body, mesh.shape["tile"], mesh.shape["orient"]),
        mesh=mesh,
        in_specs=placed,
        out_specs=(P("tile", None, None), P("tile", None, None)),
        check_vma=False,
    )
```
